128 devices in a mesh: grp: 4 (over y), slab: 32 (over z, x, core).
Axes of the slice: x: 4, y: 4, z: 4, core: 2. Of those that a mesh axis runs over, the one named last changes fastest.
Arguments:
- charges: float32 [524288], P(('grp', 'slab')), may hold values from -6 to 6
- projection: float32 [16384, 64, 64], P(('grp', 'slab')), may hold values from -0.75 to 0.75
- stencil_block: int32 [16384], P(('grp', 'slab')), may hold values from 0 to 63
- stencil_dest: int32 [16384, 1], P(('grp', 'slab')), may hold values from 0 to 127; in each aligned block of 128 rows (0 to 127, 128 to 255, ...) at most 2 rows name the same one
- stencil_cells: int32 [32768, 64], P(('grp', 'slab')), may hold values from 0 to 131071
- green_spectrum: float32 [512, 512, 512], P(('grp', 'slab')), may hold values from 2 to 330, as said below
- near_blocks: float32 [32768, 64, 64], P(('grp', 'slab')), may hold values from -0.375 to 0.375
- near_target: int32 [32768], P(('grp', 'slab')), may hold values from 0 to 63
- near_source: int32 [32768], P(('grp', 'slab')), may hold values from 0 to 191
Outputs:
- potential: float32 [524288], P(('grp', 'slab'))
The draws below stay inside these ranges and needn't reach their ends.
Inputs may be any that keep to these rules, and one draw needn't show every extreme that they name: `stencil_dest`: among the rows of one device (aligned blocks of 128 rows) at most 2 name the same device, and in some such block one device is named exactly 2 times. `green_spectrum`: Positive, and unchanged when any one frequency index f of a dimension of length L is replaced by (L - f) mod L.
All inputs are finite; a program needn't handle non-finite values.
Results may differ from the reference program's by a relative error of at most 0.00005.
Values sent between devices are 32-bit elements; how exact they have to be, the bound alone decides.
A program may use at most 64 MiB of HBM per device.

```python
import math
import jax
import jax.numpy as jnp
import numpy as np
from jax import lax

GX = 256
GY = 256
GZ = 256
BLK = 64
STEN = 64
PB_DEV = 64
SB_DEV = 128
CAP = 2
PANELS = 524288
SBLOCKS = 16384
NEARS = 32768
N_GRP = 4
N_SLAB = 32
DEVICES = 128


def folded(length):
    positions = jnp.arange(length, dtype=jnp.int32)
    return jnp.minimum(positions, length - positions)


def symbol(length):
    angle = folded(length).astype(jnp.float32) * (math.pi / length)
    sine = 2.0 * jnp.sin(angle)
    return sine * sine


def draw_green_spectrum(key, part):
    coarse_shape = (GZ + 1, GX + 1, GY + 1)
    coarse = jnp.exp(jax.random.uniform(key, coarse_shape, jnp.float32, -0.6931, 0.6931))
    strength = 1.0
    factor_field = coarse[folded(2 * GZ)][:, folded(2 * GX)][:, :, folded(2 * GY)]
    symbol_sum = symbol(2 * GZ)[:, None, None] + symbol(2 * GX)[None, :, None] + symbol(2 * GY)[None, None, :]
    return 4.0 * factor_field * (1.0 + strength / (symbol_sum + 0.05))


def touch_ends(drawn, key, least, largest):
    shape = drawn.shape
    spot = [jax.random.randint(jax.random.fold_in(key, axis), (), 0, shape[axis]) for axis in range(len(shape))]
    drawn = drawn.at[tuple(spot)].set(least)
    longest = shape.index(max(shape))
    spot[longest] = (spot[longest] + 1) % shape[longest]
    return drawn.at[tuple(spot)].set(largest)


def level_of(own_key, extent, cuts, low, largest):
    def one(position, shards_of):
        steps = jax.random.uniform(jax.random.fold_in(jax.random.fold_in(own_key, 6), position), (shards_of,), jnp.float32, low / len(cuts), largest / len(cuts))
        return jnp.repeat(jnp.exp(steps), extent[position] // shards_of).reshape((-1,) + (1,) * (len(extent) - position - 1))

    loudness = one(*cuts[0])
    for cut in cuts[1:]:
        loudness = loudness * one(*cut)
    return loudness


def routed_block(rng, own, number, rows, number_of, top, reach, skew):
    sequence = jax.random.permutation(rng, number_of)
    packed, common = portions_of(number_of, rows * top, reach, skew, True), portions_of(number_of, rows * top, reach, skew, False)
    places = jnp.arange(number_of)

    def named(tallies, turn):
        used = int((tallies > 0).sum())
        fixed = max(1, used // 4)
        moved = fixed + (places - fixed + turn * (used - fixed)) % max(1, number_of - fixed)
        return jnp.zeros((number_of,), jnp.int32).at[sequence[jnp.where(places < fixed, places, moved)]].set(jnp.asarray(tallies, jnp.int32))

    tallies = jnp.where(number % 4 == 0, named(packed, number // 4), named(common, number - number // 4 - 1))
    mixed = jax.random.permutation(jax.random.fold_in(own, 3), number_of)
    source_of, sink = mixed[0:number_of // 2 * 2:2], mixed[1:number_of // 2 * 2:2]
    slack = jnp.minimum(tallies[source_of] - 1, reach - tallies[sink]) // 2
    slack = jnp.where((source_of == sequence[0]) | (sink == sequence[0]) | (tallies[sink] == 0), 0, jnp.maximum(slack, 0))
    moved = jax.random.randint(jax.random.fold_in(own, 4), (number_of // 2,), 0, 1 << 20) % (slack + 1)
    tallies = tallies.at[source_of].add(-moved).at[sink].add(moved)
    items = jnp.searchsorted(jnp.cumsum(tallies), jnp.arange(rows * top), side="right").astype(jnp.int32)
    table = items.reshape(top, rows).T
    table = table[jax.random.permutation(jax.random.fold_in(own, 1), rows)]
    turn = jax.random.randint(jax.random.fold_in(own, 2), (rows, 1), 0, top)
    return jnp.take_along_axis(table, (jnp.arange(top)[None, :] + turn) % top, axis=1)


def portions_of(count, total, bound, skew, full):
    weights = [(1 << 20) // math.isqrt(standing ** skew) + 1 for standing in range(1, count + 1)]
    largest = bound if full else min(bound, max(-(-total // count), total * weights[0] // sum(weights)))
    least = 1 if total - largest >= count - 1 else 0
    holding, surplus = [largest] + [least] * (count - 1), total - largest - least * (count - 1)
    while surplus > 0:
        movable = [i for i in range(1, count) if holding[i] < largest] or [i for i in range(1, count) if holding[i] < bound]
        pool, left = sum([weights[i] for i in movable]), surplus
        for i in movable:
            extra = min(bound - holding[i], max(1, left * weights[i] // pool), surplus)
            holding[i] = holding[i] + extra
            surplus = surplus - extra
    return np.array(holding)


def scatter_about(rng, shape, deviation, reach, pieces=(), held_as=jnp.bfloat16):
    result = jax.random.normal(rng, shape, jnp.float32) * deviation
    if len(pieces) > 0:
        result = level_of(rng, shape, pieces, -0.22, 0.18) * result
    return jnp.clip(result, min=-reach, max=reach).astype(held_as)


def setup_inputs(seed: int = 0) -> dict:
    keys = jax.random.split(jax.random.key(seed), 10)
    charges = scatter_about(keys[0], (PANELS,), 1.0, 6.0, ((0, 128),), jnp.float32)
    projection = scatter_about(keys[1], (SBLOCKS, STEN, BLK), BLK ** -0.5, 0.75, ((0, 128),), jnp.float32)
    stencil_block = touch_ends(jax.random.randint(keys[2], (SBLOCKS,), 0, PB_DEV), jax.random.fold_in(keys[2], 1), 0, PB_DEV - 1).astype(jnp.int32)
    stencil_dest_keys = jax.random.split(jax.random.fold_in(keys[3], 1), SBLOCKS // SB_DEV)
    stencil_dest_turns = jax.random.permutation(jax.random.fold_in(keys[3], 3), SBLOCKS // SB_DEV)
    stencil_dest = jax.vmap(lambda own, number: routed_block(jax.random.fold_in(keys[3], 2), own, number, SB_DEV, DEVICES, 1, CAP, 2))(stencil_dest_keys, stencil_dest_turns).reshape((SBLOCKS, 1))
    stencil_cells = touch_ends(jax.random.randint(keys[4], (DEVICES * DEVICES * CAP, STEN), 0, (GX // DEVICES) * GY * GZ), jax.random.fold_in(keys[4], 1), 0, ((GX // DEVICES) * GY * GZ) - 1).astype(jnp.int32)
    green_spectrum = draw_green_spectrum(jax.random.fold_in(keys[9], 71), 0)
    near_blocks = scatter_about(keys[6], (NEARS, BLK, BLK), (4 * BLK) ** -0.5, 0.375, ((0, 128),), jnp.float32)
    near_target = touch_ends(jax.random.randint(keys[7], (NEARS,), 0, PB_DEV), jax.random.fold_in(keys[7], 1), 0, PB_DEV - 1).astype(jnp.int32)
    near_source = touch_ends(jax.random.randint(keys[8], (NEARS,), 0, 3 * PB_DEV), jax.random.fold_in(keys[8], 1), 0, (3 * PB_DEV) - 1).astype(jnp.int32)
    return {"charges": charges, "projection": projection, "stencil_block": stencil_block, "stencil_dest": stencil_dest, "stencil_cells": stencil_cells, "green_spectrum": green_spectrum, "near_blocks": near_blocks, "near_target": near_target, "near_source": near_source}


def reference(charges, projection, stencil_block, stencil_dest, stencil_cells, green_spectrum, near_blocks, near_target, near_source):
    devices = N_GRP * N_SLAB
    planes_dev = GX // devices
    cells_dev = planes_dev * GY * GZ
    capacity = stencil_cells.shape[0] // (devices * devices)
    panel_rows = charges.reshape(devices * PB_DEV, BLK)
    sblocks = stencil_block.shape[0]
    per_device = sblocks // devices
    source = (jnp.arange(sblocks, dtype=jnp.int32) // per_device).astype(jnp.int32)
    owning = source * PB_DEV + stencil_block
    values = jnp.einsum('bsp,bp->bs', projection, panel_rows[owning], precision=lax.Precision.HIGHEST)
    target = stencil_dest[:, 0]
    grouped = target.reshape(devices, per_device)
    matches = (grouped[:, :, None] == jnp.arange(devices, dtype=jnp.int32)[None, None, :]).astype(jnp.int32)
    ranking = (jnp.sum(jnp.cumsum(matches, axis=1) * matches, axis=2) - 1).reshape(-1).astype(jnp.int32)
    slot_row = (target * (devices * capacity) + source * capacity + ranking).astype(jnp.int32)
    cell_index = (target[:, None] * cells_dev + stencil_cells[slot_row]).astype(jnp.int32)
    grid_flat = jnp.zeros((GX * GY * GZ,), jnp.float32).at[cell_index.reshape(-1)].add(values.reshape(-1))
    padded = jnp.zeros((2 * GX, 2 * GY, 2 * GZ), jnp.float32).at[:GX, :GY, :GZ].set(grid_flat.reshape(GX, GY, GZ))
    spectrum = jnp.transpose(green_spectrum, (1, 2, 0))[:, :, :GZ + 1]
    potential_grid = jnp.fft.irfftn(jnp.fft.rfftn(padded) * spectrum, s=padded.shape)[:GX, :GY, :GZ]
    sampled = potential_grid.reshape(-1)[cell_index]
    far_terms = jnp.einsum('bsp,bs->bp', projection, sampled, precision=lax.Precision.HIGHEST)
    far_field = jnp.zeros((devices * PB_DEV, BLK), jnp.float32).at[owning].add(far_terms)
    nears = near_target.shape[0]
    near_per = nears // devices
    near_owner = (jnp.arange(nears, dtype=jnp.int32) // near_per).astype(jnp.int32)
    global_source = (near_owner * PB_DEV + near_source - PB_DEV).astype(jnp.int32)
    usable = (global_source >= 0) & (global_source < devices * PB_DEV)
    picked = panel_rows[jnp.clip(global_source, 0, devices * PB_DEV - 1)]
    sources = jnp.where(usable[:, None], picked, jnp.zeros_like(picked))
    near_terms = jnp.einsum('nij,nj->ni', near_blocks, sources, precision=lax.Precision.HIGHEST)
    near_field = jnp.zeros((devices * PB_DEV, BLK), jnp.float32).at[near_owner * PB_DEV + near_target].add(near_terms)
    return (far_field + near_field).reshape(-1)
```

```python
import math

import jax
import jax.numpy as jnp
from jax import lax
from jax.sharding import PartitionSpec as P

GX = 256
GY = 256
GZ = 256
BLK = 64
STEN = 64


highest = lax.Precision.HIGHEST


def with_halo(x, sides, width):
    for axis, dim in sides:
        devices, length = (lax.axis_size(axis), x.shape[dim])
        up = [(i, (i + 1) % devices) for i in range(devices - 1)]
        down = [(j, i) for i, j in up]
        last = lax.slice_in_dim(x, length - width, length, axis=dim)
        first = lax.slice_in_dim(x, 0, width, axis=dim)
        before = lax.ppermute(last, axis, up)
        after = lax.ppermute(first, axis, down)
        x = jnp.concatenate([before, x, after], axis=dim)
    return x


def cas_table(in_count, out_count, length):
    first_index = jnp.arange(in_count, dtype=jnp.int32)[:, None]
    second_index = jnp.arange(out_count, dtype=jnp.int32)[None, :]
    phase = (first_index * second_index % length).astype(jnp.float32) * (2.0 * math.pi / length)
    return jnp.cos(phase) + jnp.sin(phase)


def one_hot_rows(indices, count):
    return (indices[:, None] == jnp.arange(count, dtype=jnp.int32)[None, :]).astype(jnp.float32)


def halves(x):
    top = lax.reduce_precision(x, 8, 7)
    return top.astype(jnp.bfloat16), (x - top).astype(jnp.bfloat16)


def one_hot_cols(indices, count):
    return indices[None, :] == jnp.arange(count, dtype=jnp.int32)[:, None]


def spread(cell_list, amounts, height, width):
    rows = one_hot_cols(cell_list // width, height).astype(jnp.bfloat16)
    cols = one_hot_cols(cell_list % width, width)
    zero = jnp.zeros((), jnp.bfloat16)
    weighted = jnp.concatenate([jnp.where(cols, part[None, :], zero) for part in halves(amounts)], axis=0)
    both = lax.dot_general(weighted, rows, (((1,), (1,)), ((), ())), preferred_element_type=jnp.float32)
    return both[:width] + both[width:]


def sample(cell_list, grid_cols):
    width, height = grid_cols.shape
    rows = one_hot_cols(cell_list // width, height).astype(jnp.bfloat16)
    cols = one_hot_cols(cell_list % width, width)
    both = jnp.dot(jnp.concatenate(halves(grid_cols), axis=0), rows, preferred_element_type=jnp.float32)
    return jnp.sum(jnp.where(cols, both[:width] + both[width:], 0.0), axis=0)


def convolve(slab_grid, green_spectrum):
    z_length = 2 * GZ
    x_length = 2 * GX
    y_length = 2 * GY
    high = lax.Precision.HIGH
    planes = jnp.einsum("zxy,zw->wxy", slab_grid, cas_table(GZ, z_length, z_length), precision=high)
    pencils = lax.all_to_all(planes, ("grp", "slab"), split_axis=0, concat_axis=1, tiled=True)
    spectral = jnp.einsum("wxy,xu->wuy", pencils, cas_table(GX, x_length, x_length), precision=high)
    spectral = jnp.einsum("wuy,yv->wuv", spectral, cas_table(GY, y_length, y_length), precision=high)
    product = spectral * green_spectrum
    back = jnp.einsum("wuv,vy->wuy", product, cas_table(y_length, GY, y_length), precision=high)
    back = jnp.einsum("wuy,ux->wxy", back, cas_table(x_length, GX, x_length), precision=high)
    slabs = lax.all_to_all(back, ("grp", "slab"), split_axis=1, concat_axis=0, tiled=True)
    result = jnp.einsum("wxy,wz->zxy", slabs, cas_table(z_length, GZ, z_length), precision=high)
    return result / float(z_length * x_length * y_length)


def per_device(
    charges,
    projection,
    stencil_block,
    stencil_dest,
    stencil_cells,
    green_spectrum,
    near_blocks,
    near_target,
    near_source,
):
    devices = lax.axis_size(("grp", "slab"))
    sblocks = stencil_block.shape[0]
    capacity = stencil_cells.shape[0] // devices
    panel_rows = charges.reshape(-1, BLK)
    pblocks = panel_rows.shape[0]
    owning = one_hot_rows(stencil_block, pblocks)
    gathered = jnp.dot(owning, panel_rows, precision=highest)
    values = jnp.einsum("bsp,bp->bs", projection, gathered, precision=highest)
    target = stencil_dest[:, 0]
    matches = one_hot_rows(target, devices)
    triangle = (jnp.arange(sblocks)[:, None] >= jnp.arange(sblocks)[None, :]).astype(jnp.float32)
    running = jnp.dot(triangle, matches, precision=highest)
    ranking = (jnp.sum(running * matches, axis=1) - 1.0).astype(jnp.int32)
    position = target * capacity + ranking
    placing = (
        jnp.arange(devices * capacity, dtype=jnp.int32)[:, None] == position[None, :]
    ).astype(jnp.float32)
    outgoing = jnp.dot(placing, values, precision=highest).reshape(devices, capacity * STEN)
    incoming = lax.all_to_all(outgoing, ("grp", "slab"), split_axis=0, concat_axis=0, tiled=True)
    cell_list = stencil_cells.reshape(-1)
    planes_dev = GX // devices
    slab_grid = spread(cell_list, incoming.reshape(-1), planes_dev * GY, GZ)
    potential_grid = convolve(slab_grid.reshape(GZ, planes_dev, GY), green_spectrum)
    sampled = sample(cell_list, potential_grid.reshape(GZ, planes_dev * GY)).reshape(
        devices, capacity * STEN
    )
    returned = lax.all_to_all(
        sampled, ("grp", "slab"), split_axis=0, concat_axis=0, tiled=True
    ).reshape(devices * capacity, STEN)
    at_stencil = lax.dot_general(placing, returned, (((0,), (0,)), ((), ())), precision=highest)
    far_terms = jnp.einsum("bsp,bs->bp", projection, at_stencil, precision=highest)
    far_field = lax.dot_general(owning, far_terms, (((0,), (0,)), ((), ())), precision=highest)
    extended = with_halo(charges, ((("grp", "slab"), 0),), charges.shape[0]).reshape(-1, BLK)
    sources = jnp.dot(one_hot_rows(near_source, extended.shape[0]), extended, precision=highest)
    near_terms = jnp.einsum("nij,nj->ni", near_blocks, sources, precision=highest)
    receiver = (jnp.arange(pblocks, dtype=jnp.int32)[:, None] == near_target[None, :]).astype(
        jnp.float32
    )
    near_field = jnp.dot(receiver, near_terms, precision=highest)
    return (far_field + near_field).reshape(-1)


def solution(mesh):
    placed = (
        P(("grp", "slab")),
        P(("grp", "slab"), None, None),
        P(("grp", "slab")),
        P(("grp", "slab"), None),
        P(("grp", "slab"), None),
        P(("grp", "slab"), None, None),
        P(("grp", "slab"), None, None),
        P(("grp", "slab")),
        P(("grp", "slab")),
    )
    return jax.shard_map(
        per_device, mesh=mesh, in_specs=placed, out_specs=P(("grp", "slab")), check_vma=False
    )
```

```python
import functools
import math

import jax
import jax.numpy as jnp
import numpy as np
from jax import lax
from jax.experimental import pallas as pl
from jax.experimental.pallas import tpu as pltpu
from jax.sharding import PartitionSpec as P

GX = 256
GY = 256
GZ = 256
BLK = 64
STEN = 64
LANES = 128


highest = lax.Precision.HIGHEST
NN = (((1,), (0,)), ((), ()))
NT = (((1,), (1,)), ((), ()))


def with_halo(x, sides, width):
    for axis, dim in sides:
        devices, length = (lax.axis_size(axis), x.shape[dim])
        up = [(i, (i + 1) % devices) for i in range(devices - 1)]
        down = [(j, i) for i, j in up]
        last = lax.slice_in_dim(x, length - width, length, axis=dim)
        first = lax.slice_in_dim(x, 0, width, axis=dim)
        before = lax.ppermute(last, axis, up)
        after = lax.ppermute(first, axis, down)
        x = jnp.concatenate([before, x, after], axis=dim)
    return x


def one_hot_rows(indices, count):
    return (indices[:, None] == jnp.arange(count, dtype=jnp.int32)[None, :]).astype(jnp.float32)


def cas_table(rows, columns, length):
    phase = np.outer(np.arange(rows), np.arange(columns)) % length * (2.0 * math.pi / length)
    return (np.cos(phase) + np.sin(phase)).astype(np.float32)


def lane_parts(table):
    return np.stack(np.split(table, table.shape[1] // LANES, axis=1))


def halves(x):
    top = x.astype(jnp.bfloat16)
    return top, (x - top.astype(jnp.float32)).astype(jnp.bfloat16)


def product(left, right, form):
    def one(a, b):
        return lax.dot_general(a, b, form, preferred_element_type=jnp.float32)

    return one(left[0], right[0]) + one(left[0], right[1]) + one(left[1], right[0])


def whole_kernel(
    devices, slab, values, cells, table, table_t, green_hbm, out,
    rows_hot, cols_hot, weighted, grid_sum, tall, wide, green, left, mid, line, pot,
    recv1, send2, recv2, send3, recv3, send4, recv4, sends, recvs, green_sem,
):
    me = lax.axis_index("grp") * slab + lax.axis_index("slab")
    half = devices

    def place(k):
        p = lax.rem(me + k, devices)
        return p, (p // slab, lax.rem(p, slab))

    barrier = pltpu.get_barrier_semaphore()

    def greet(k, carry):
        pl.semaphore_signal(barrier, inc=1, device_id=place(k)[1], device_id_type=pl.DeviceIdType.MESH)
        return carry

    lax.fori_loop(1, devices, greet, 0)
    green_copy = pltpu.make_async_copy(green_hbm, green, green_sem)
    green_copy.start()

    for h in range(2):
        lanes = slice(h * LANES, (h + 1) * LANES)
        tall[0, :, lanes], tall[1, :, lanes] = halves(table[h])
        for j in range(4):
            block = table.at[h][pl.ds(j, half, stride=4), :]
            rows = slice(j * half, (j + 1) * half)
            tall[2, rows, lanes], tall[3, rows, lanes] = halves(block)
            wide[0, lanes, rows], wide[1, lanes, rows] = halves(block.T)
    for q in range(4):
        lanes = slice(q * LANES, (q + 1) * LANES)
        for xx in range(2):
            block = table_t.at[q][pl.ds(xx, half, stride=2), :]
            rows = slice(xx * half, (xx + 1) * half)
            wide[2, rows, lanes], wide[3, rows, lanes] = halves(block)
            tall[4, lanes, rows], tall[5, lanes, rows] = halves(block.T)

    pl.semaphore_wait(barrier, devices - 1)

    def row_of(ref, p):
        return ref.at[p]

    def tile_of(ref, p):
        return ref.at[:, pl.ds(pl.multiple_of(p * 8, 8), 8), :]

    def start_all(number, source, target, view):
        def start(k, carry):
            p, where = place(k)
            pltpu.make_async_remote_copy(
                src_ref=view(source, p), dst_ref=view(target, me),
                send_sem=sends.at[number], recv_sem=recvs.at[number],
                device_id=where, device_id_type=pl.DeviceIdType.MESH,
            ).start()
            return carry

        lax.fori_loop(1, devices, start, 0)

    def wait_all(ref, sem, view):
        part = ref.at[pl.ds(0, devices - 1)] if view is row_of else ref.at[:, pl.ds(0, (devices - 1) * 8), :]
        pltpu.make_async_copy(part, part, sem).wait()

    start_all(0, values, recv1, row_of)
    recv1[me] = values[me]

    row_id = lax.broadcasted_iota(jnp.int32, (2 * GY, LANES), 0)
    col_id = lax.broadcasted_iota(jnp.int32, (GZ, LANES), 0)

    def mark(e, carry):
        c = e // 8
        lanes = pl.ds(pl.multiple_of(lax.rem(e, 8) * LANES, LANES), LANES)
        cell = cells[e]
        row = lax.shift_right_logical(cell, 8)
        col = lax.bitwise_and(cell, 255)
        rows_hot[c, :, lanes] = jnp.where(row_id == row, 1.0, 0.0).astype(jnp.bfloat16)
        cols_hot[c, :, lanes] = jnp.where(col_id == col, 1.0, 0.0).astype(jnp.bfloat16)
        return carry

    lax.fori_loop(0, devices, mark, 0)
    wait_all(recv1, recvs.at[0], row_of)

    grid_sum[...] = jnp.zeros_like(grid_sum)

    def spread(c, carry):
        for k in range(8):
            lanes = slice(k * LANES, (k + 1) * LANES)
            hot = cols_hot[c, :, lanes]
            top, rest = halves(jnp.broadcast_to(recv1[c * 8 + k], (GZ, LANES)))
            weighted[0:GZ, lanes] = hot * top
            weighted[GZ:, lanes] = hot * rest
        grid_sum[...] += lax.dot_general(weighted[...], rows_hot[c], NT, preferred_element_type=jnp.float32)
        return carry

    lax.fori_loop(0, devices // 8, spread, 0)

    for xx in range(2):
        part = slice(xx * GY, (xx + 1) * GY)
        grid = halves(grid_sum[0:GZ, part] + grid_sum[GZ:, part])
        for j in range(4):
            rows = slice(j * half, (j + 1) * half)
            planes = product((tall[2, rows], tall[3, rows]), grid, NN)
            for h in range(2):
                send2.at[h][pl.ds(2 * j + xx, half, stride=8), :] = planes[:, h * LANES:(h + 1) * LANES]

    start_all(1, send2, recv2, tile_of)
    mine = pl.ds(pl.multiple_of(me * 8, 8), 8)
    recv2[:, mine, :] = send2[:, mine, :]
    green_copy.wait()
    wait_all(recv2, recvs.at[1], tile_of)

    for j in range(4):
        for h in range(2):
            lanes = slice(h * LANES, (h + 1) * LANES)
            for xx in range(2):
                rows = slice(xx * half, (xx + 1) * half)
                piece = recv2.at[h][pl.ds(2 * j + xx, half, stride=8), :]
                left[0, rows, lanes], left[1, rows, lanes] = halves(piece)
        line[...] = jnp.zeros_like(line)

        def convolve(b, carry):
            rows = pl.ds(pl.multiple_of(b * 256, 256), 256)
            along_x = halves(product((tall[4, rows], tall[5, rows]), (left[0], left[1]), NN))
            spectral = product(along_x, (tall[0], tall[1]), NT)
            scaled = halves(spectral * green[j, rows, :])
            back_y = halves(product(scaled, (tall[0], tall[1]), NN))
            line[...] += product((wide[2, :, rows], wide[3, :, rows]), back_y, NN)
            return carry

        lax.fori_loop(0, 2, convolve, 0)
        for h in range(2):
            for xx in range(2):
                send3.at[h][pl.ds(2 * j + xx, half, stride=8), :] = line[xx * half:(xx + 1) * half, h * LANES:(h + 1) * LANES]

    start_all(2, send3, recv3, tile_of)
    recv3[:, mine, :] = send3[:, mine, :]
    wait_all(recv3, recvs.at[2], tile_of)

    scale = 1.0 / float(8 * GX * GY * GZ)
    for xx in range(2):
        for j in range(4):
            rows = slice(j * half, (j + 1) * half)
            for h in range(2):
                lanes = slice(h * LANES, (h + 1) * LANES)
                piece = recv3.at[h][pl.ds(2 * j + xx, half, stride=8), :]
                mid[0, rows, lanes], mid[1, rows, lanes] = halves(piece)
        top, rest = halves(product((wide[0], wide[1]), (mid[0], mid[1]), NN) * scale)
        part = slice(xx * GY, (xx + 1) * GY)
        pot[0:GZ, part] = top
        pot[GZ:, part] = rest

    def sample(c, carry):
        for k in range(4):
            lanes = slice(k * 256, (k + 1) * 256)
            read = lax.dot_general(pot[...], rows_hot[c, :, lanes], NN, preferred_element_type=jnp.float32)
            kept = (read[0:GZ] + read[GZ:]) * cols_hot[c, :, lanes].astype(jnp.float32)
            total = jnp.sum(kept, axis=0, keepdims=True)
            for i in range(2):
                send4[c * 8 + 2 * k + i] = total[:, i * LANES:(i + 1) * LANES]
        return carry

    lax.fori_loop(0, devices // 8, sample, 0)

    start_all(3, send4, recv4, row_of)
    recv4[me] = send4[me]
    wait_all(recv4, recvs.at[3], row_of)
    out[...] = recv4[...]
    for number, (ref, view) in enumerate(((values, row_of), (send2, tile_of), (send3, tile_of), (send4, row_of))):
        wait_all(ref, sends.at[number], view)


def far_grid(outgoing, stencil_cells, green_spectrum, devices, slab):
    table = cas_table(2 * GZ, GZ, 2 * GZ)
    vmem = pl.BlockSpec(memory_space=pltpu.VMEM)
    f32, bf16 = jnp.float32, jnp.bfloat16
    rows = devices * 8
    return pl.pallas_call(
        functools.partial(whole_kernel, devices, slab),
        out_shape=jax.ShapeDtypeStruct((devices, 1, LANES), f32),
        in_specs=[vmem, vmem, vmem, vmem, pl.BlockSpec(memory_space=pl.ANY)],
        out_specs=vmem,
        scratch_shapes=[
            pltpu.VMEM((devices // 8, 2 * GY, 8 * LANES), bf16),
            pltpu.VMEM((devices // 8, GZ, 8 * LANES), bf16),
            pltpu.VMEM((2 * GZ, 8 * LANES), bf16),
            pltpu.VMEM((2 * GZ, 2 * GY), f32),
            pltpu.VMEM((6, 2 * GZ, GZ), bf16),
            pltpu.VMEM((4, GZ, 2 * GZ), bf16),
            pltpu.VMEM((4, 2 * GX, 2 * GY), f32),
            pltpu.VMEM((2, GX, GY), bf16),
            pltpu.VMEM((2, 2 * GZ, GY), bf16),
            pltpu.VMEM((GX, GY), f32),
            pltpu.VMEM((2 * GZ, 2 * GY), bf16),
            pltpu.VMEM((devices, 1, LANES), f32),
            pltpu.VMEM((2, rows, LANES), f32),
            pltpu.VMEM((2, rows, LANES), f32),
            pltpu.VMEM((2, rows, LANES), f32),
            pltpu.VMEM((2, rows, LANES), f32),
            pltpu.VMEM((devices, 1, LANES), f32),
            pltpu.VMEM((devices, 1, LANES), f32),
            pltpu.SemaphoreType.DMA((4,)),
            pltpu.SemaphoreType.DMA((4,)),
            pltpu.SemaphoreType.DMA,
        ],
        compiler_params=pltpu.CompilerParams(
            collective_id=0, has_side_effects=True, vmem_limit_bytes=58 * 1024 * 1024
        ),
    )(outgoing, stencil_cells, jnp.asarray(lane_parts(table)), jnp.asarray(lane_parts(table.T)), green_spectrum)


def per_device(
    charges,
    projection,
    stencil_block,
    stencil_dest,
    stencil_cells,
    green_spectrum,
    near_blocks,
    near_target,
    near_source,
):
    devices = lax.axis_size(("grp", "slab"))
    sblocks = stencil_block.shape[0]
    capacity = stencil_cells.shape[0] // devices
    panel_rows = charges.reshape(-1, BLK)
    pblocks = panel_rows.shape[0]
    owning = one_hot_rows(stencil_block, pblocks)
    gathered = jnp.dot(owning, panel_rows, precision=highest)
    values = jnp.einsum("bsp,bp->bs", projection, gathered, precision=highest)
    target = stencil_dest[:, 0]
    matches = one_hot_rows(target, devices)
    triangle = (jnp.arange(sblocks)[:, None] >= jnp.arange(sblocks)[None, :]).astype(jnp.float32)
    running = jnp.dot(triangle, matches, precision=highest)
    ranking = (jnp.sum(running * matches, axis=1) - 1.0).astype(jnp.int32)
    position = target * capacity + ranking
    placing = (
        jnp.arange(devices * capacity, dtype=jnp.int32)[:, None] == position[None, :]
    ).astype(jnp.float32)
    outgoing = jnp.dot(placing, values, precision=highest).reshape(devices, 1, capacity * STEN)
    cell_rows = stencil_cells.reshape(devices, 1, capacity * STEN)
    slab = lax.axis_size("slab")
    returned = far_grid(outgoing, cell_rows, green_spectrum, devices, slab).reshape(devices * capacity, STEN)
    at_stencil = lax.dot_general(placing, returned, (((0,), (0,)), ((), ())), precision=highest)
    far_terms = jnp.einsum("bsp,bs->bp", projection, at_stencil, precision=highest)
    far_field = lax.dot_general(owning, far_terms, (((0,), (0,)), ((), ())), precision=highest)
    extended = with_halo(charges, ((("grp", "slab"), 0),), charges.shape[0]).reshape(-1, BLK)
    sources = jnp.dot(one_hot_rows(near_source, extended.shape[0]), extended, precision=highest)
    near_terms = jnp.einsum("nij,nj->ni", near_blocks, sources, precision=highest)
    receiver = (jnp.arange(pblocks, dtype=jnp.int32)[:, None] == near_target[None, :]).astype(
        jnp.float32
    )
    near_field = jnp.dot(receiver, near_terms, precision=highest)
    return (far_field + near_field).reshape(-1)


def solution(mesh):
    placed = (
        P(("grp", "slab")),
        P(("grp", "slab"), None, None),
        P(("grp", "slab")),
        P(("grp", "slab"), None),
        P(("grp", "slab"), None),
        P(("grp", "slab"), None, None),
        P(("grp", "slab"), None, None),
        P(("grp", "slab")),
        P(("grp", "slab")),
    )
    return jax.shard_map(
        per_device, mesh=mesh, in_specs=placed, out_specs=P(("grp", "slab")), check_vma=False
    )
```

```python
import functools
import math

import jax
import jax.numpy as jnp
import numpy as np
from jax import lax
from jax.experimental import pallas as pl
from jax.experimental.pallas import tpu as pltpu
from jax.sharding import PartitionSpec as P

GX = 256
GY = 256
GZ = 256
BLK = 64
STEN = 64
LANES = 128


highest = lax.Precision.HIGHEST
NN = (((1,), (0,)), ((), ()))
NT = (((1,), (1,)), ((), ()))


def with_halo(x, sides, width):
    for axis, dim in sides:
        devices, length = (lax.axis_size(axis), x.shape[dim])
        up = [(i, (i + 1) % devices) for i in range(devices - 1)]
        down = [(j, i) for i, j in up]
        last = lax.slice_in_dim(x, length - width, length, axis=dim)
        first = lax.slice_in_dim(x, 0, width, axis=dim)
        before = lax.ppermute(last, axis, up)
        after = lax.ppermute(first, axis, down)
        x = jnp.concatenate([before, x, after], axis=dim)
    return x


def one_hot_rows(indices, count):
    return (indices[:, None] == jnp.arange(count, dtype=jnp.int32)[None, :]).astype(jnp.float32)


def cas_table(rows, columns, length):
    phase = np.outer(np.arange(rows), np.arange(columns)) % length * (2.0 * math.pi / length)
    return (np.cos(phase) + np.sin(phase)).astype(np.float32)


def lane_parts(table):
    return np.stack(np.split(table, table.shape[1] // LANES, axis=1))


def halves(x):
    top = x.astype(jnp.bfloat16)
    return top, (x - top.astype(jnp.float32)).astype(jnp.bfloat16)


def product(left, right, form):
    def one(a, b):
        return lax.dot_general(a, b, form, preferred_element_type=jnp.float32)

    return one(left[0], right[0]) + one(left[0], right[1]) + one(left[1], right[0])


def whole_kernel(
    devices, slab, values, cells, table, table_t, green_hbm, out,
    rows_hot, cols_hot, weighted, weighted_next, grid_sum, tall, wide, green, left, right, mid, pot,
    recv1, send2a, send2b, recv2a, recv2b, send3a, send3b, recv3a, recv3b, send4, recv4, sends, recvs, green_sem,
):
    send2, recv2, send3, recv3 = (send2a, send2b), (recv2a, recv2b), (send3a, send3b), (recv3a, recv3b)
    me = lax.axis_index("grp") * slab + lax.axis_index("slab")
    half = devices

    def place(k):
        p = lax.rem(me + k, devices)
        return p, (p // slab, lax.rem(p, slab))

    barrier = pltpu.get_barrier_semaphore()

    def greet(k, carry):
        pl.semaphore_signal(barrier, inc=1, device_id=place(k)[1], device_id_type=pl.DeviceIdType.MESH)
        return carry

    lax.fori_loop(1, devices, greet, 0)
    green_copy = pltpu.make_async_copy(green_hbm, green, green_sem)
    green_copy.start()

    for h in range(2):
        lanes = slice(h * LANES, (h + 1) * LANES)
        tall[0, :, lanes], tall[1, :, lanes] = halves(table[h])
        for j in range(4):
            block = table.at[h][pl.ds(j, half, stride=4), :]
            rows = slice(j * half, (j + 1) * half)
            tall[2, rows, lanes], tall[3, rows, lanes] = halves(block)
            wide[0, lanes, rows], wide[1, lanes, rows] = halves(block.T)
    for q in range(4):
        lanes = slice(q * LANES, (q + 1) * LANES)
        for xx in range(2):
            block = table_t.at[q][pl.ds(xx, half, stride=2), :]
            rows = slice(xx * half, (xx + 1) * half)
            wide[2, rows, lanes], wide[3, rows, lanes] = halves(block)
            tall[4, lanes, rows], tall[5, lanes, rows] = halves(block.T)

    pl.semaphore_wait(barrier, devices - 1)

    def row_of(ref, p):
        return ref.at[p]

    def tile_of(ref, p):
        return ref.at[pl.ds(pl.multiple_of(p * 8, 8), 8), :]

    def start_one(number, source, target, view, k):
        p, where = place(k)
        pltpu.make_async_remote_copy(
            src_ref=view(source, p), dst_ref=view(target, me),
            send_sem=sends.at[number], recv_sem=recvs.at[number],
            device_id=where, device_id_type=pl.DeviceIdType.MESH,
        ).start()

    def start_all(number, source, target):
        def start(k, carry):
            start_one(number, source, target, tile_of, k)
            return carry

        lax.fori_loop(1, devices, start, 0)

    def wait_all(ref, sem, view):
        part = ref.at[pl.ds(0, devices - 1)] if view is row_of else ref.at[pl.ds(0, (devices - 1) * 8), :]
        pltpu.make_async_copy(part, part, sem).wait()

    row_id = lax.broadcasted_iota(jnp.int32, (2 * GY, LANES), 0)
    col_id = lax.broadcasted_iota(jnp.int32, (GZ, LANES), 0)

    def mark(e):
        c = e // 8
        lanes = pl.ds(pl.multiple_of(lax.rem(e, 8) * LANES, LANES), LANES)
        cell = cells[e]
        row = lax.shift_right_logical(cell, 8)
        col = lax.bitwise_and(cell, 255)
        rows_hot[c, :, lanes] = jnp.where(row_id == row, 1.0, 0.0).astype(jnp.bfloat16)
        cols_hot[c, :, lanes] = jnp.where(col_id == col, 1.0, 0.0).astype(jnp.bfloat16)

    def send_and_mark(k, carry):
        start_one(0, values, recv1, row_of, k)
        mark(k)
        return carry

    lax.fori_loop(1, devices, send_and_mark, 0)
    mark(0)
    recv1[me] = values[me]
    wait_all(recv1, recvs.at[0], row_of)

    def weigh(c, into):
        for k in range(8):
            lanes = slice(k * LANES, (k + 1) * LANES)
            hot = cols_hot[c, :, lanes]
            top, rest = halves(jnp.broadcast_to(recv1[c * 8 + k], (GZ, LANES)))
            into[0:GZ, lanes] = hot * top
            into[GZ:, lanes] = hot * rest

    def add_chunk(c, weights):
        grid_sum[...] += lax.dot_general(weights[...], rows_hot[c], NT, preferred_element_type=jnp.float32)

    grid_sum[...] = jnp.zeros_like(grid_sum)
    weigh(0, weighted)
    chunks = devices // 8

    def spread(i, carry):
        weigh(2 * i + 1, weighted_next)
        add_chunk(2 * i, weighted)
        weigh(jnp.minimum(2 * i + 2, chunks - 1), weighted)
        add_chunk(2 * i + 1, weighted_next)
        return carry

    lax.fori_loop(0, chunks // 2, spread, 0)

    mine = pl.ds(pl.multiple_of(me * 8, 8), 8)

    def spots(j, xx, h):
        return pl.ds(4 * j + 2 * xx + h, half, stride=8)

    for xx in range(2):
        part = slice(xx * GY, (xx + 1) * GY)
        left[xx], right[xx] = halves(grid_sum[0:GZ, part] + grid_sum[GZ:, part])
    for side in range(2):
        for xx in range(2):
            for j in range(2):
                rows = slice((2 * side + j) * half, (2 * side + j + 1) * half)
                planes = product((tall[2, rows], tall[3, rows]), (left[xx], right[xx]), NN)
                for h in range(2):
                    send2[side][spots(j, xx, h), :] = planes[:, h * LANES:(h + 1) * LANES]
        start_all(1 + side, send2[side], recv2[side])
        recv2[side][mine, :] = send2[side][mine, :]
    green_copy.wait()

    for side in range(2):
        wait_all(recv2[side], recvs.at[1 + side], tile_of)
        for j in range(2):
            for h in range(2):
                lanes = slice(h * LANES, (h + 1) * LANES)
                for xx in range(2):
                    rows = slice(xx * half, (xx + 1) * half)
                    left[0, rows, lanes], left[1, rows, lanes] = halves(recv2[side][spots(j, xx, h), :])
            total = None
            for b in range(2):
                rows = slice(b * GX, (b + 1) * GX)
                along_x = halves(product((tall[4, rows], tall[5, rows]), (left[0], left[1]), NN))
                spectral = product(along_x, (tall[0], tall[1]), NT)
                scaled = halves(spectral * green[2 * side + j, rows, :])
                back_y = halves(product(scaled, (tall[0], tall[1]), NN))
                term = product((wide[2, :, rows], wide[3, :, rows]), back_y, NN)
                total = term if total is None else total + term
            for h in range(2):
                for xx in range(2):
                    send3[side][spots(j, xx, h), :] = total[xx * half:(xx + 1) * half, h * LANES:(h + 1) * LANES]
        start_all(3 + side, send3[side], recv3[side])
        recv3[side][mine, :] = send3[side][mine, :]

    for side in range(2):
        wait_all(recv3[side], recvs.at[3 + side], tile_of)
        for xx in range(2):
            for j in range(2):
                rows = slice((2 * side + j) * half, (2 * side + j + 1) * half)
                for h in range(2):
                    lanes = slice(xx * GY + h * LANES, xx * GY + (h + 1) * LANES)
                    mid[0, rows, lanes], mid[1, rows, lanes] = halves(recv3[side][spots(j, xx, h), :])
    scale = 1.0 / float(8 * GX * GY * GZ)
    for xx in range(2):
        part = slice(xx * GY, (xx + 1) * GY)
        top, rest = halves(product((wide[0], wide[1]), (mid[0, :, part], mid[1, :, part]), NN) * scale)
        pot[0:GZ, part] = top
        pot[GZ:, part] = rest

    def sample(i, carry):
        c = lax.rem(me // 8 + i, chunks)
        for k in range(4):
            lanes = slice(k * 256, (k + 1) * 256)
            read = lax.dot_general(pot[...], rows_hot[c, :, lanes], NN, preferred_element_type=jnp.float32)
            kept = (read[0:GZ] + read[GZ:]) * cols_hot[c, :, lanes].astype(jnp.float32)
            total = jnp.sum(kept, axis=0, keepdims=True)
            for q in range(2):
                send4[c * 8 + 2 * k + q] = total[:, q * LANES:(q + 1) * LANES]
        return carry

    def send_chunk(i):
        c = lax.rem(me // 8 + i, chunks)
        for q in range(8):
            p = c * 8 + q

            @pl.when(p != me)
            def _():
                start_one(5, send4, recv4, row_of, lax.rem(p + devices - me, devices))

    def sample_and_send(i, carry):
        sample(i, 0)
        send_chunk(i)
        return carry

    lax.fori_loop(0, chunks, sample_and_send, 0)
    recv4[me] = send4[me]
    wait_all(recv4, recvs.at[5], row_of)
    out[...] = recv4[...]
    wait_all(values, sends.at[0], row_of)
    for side in range(2):
        wait_all(send2[side], sends.at[1 + side], tile_of)
        wait_all(send3[side], sends.at[3 + side], tile_of)
    wait_all(send4, sends.at[5], row_of)


def far_grid(outgoing, stencil_cells, green_spectrum, devices, slab):
    table = cas_table(2 * GZ, GZ, 2 * GZ)
    vmem = pl.BlockSpec(memory_space=pltpu.VMEM)
    f32, bf16 = jnp.float32, jnp.bfloat16
    rows = devices * 8
    return pl.pallas_call(
        functools.partial(whole_kernel, devices, slab),
        out_shape=jax.ShapeDtypeStruct((devices, 1, LANES), f32),
        in_specs=[vmem, vmem, vmem, vmem, pl.BlockSpec(memory_space=pl.ANY)],
        out_specs=vmem,
        scratch_shapes=[
            pltpu.VMEM((devices // 8, 2 * GY, 8 * LANES), bf16),
            pltpu.VMEM((devices // 8, GZ, 8 * LANES), bf16),
            pltpu.VMEM((2 * GZ, 8 * LANES), bf16),
            pltpu.VMEM((2 * GZ, 8 * LANES), bf16),
            pltpu.VMEM((2 * GZ, 2 * GY), f32),
            pltpu.VMEM((6, 2 * GZ, GZ), bf16),
            pltpu.VMEM((4, GZ, 2 * GZ), bf16),
            pltpu.VMEM((4, 2 * GX, 2 * GY), f32),
            pltpu.VMEM((2, GX, GY), bf16),
            pltpu.VMEM((2, GX, GY), bf16),
            pltpu.VMEM((2, 2 * GZ, 2 * GY), bf16),
            pltpu.VMEM((2 * GZ, 2 * GY), bf16),
            pltpu.VMEM((devices, 1, LANES), f32),
            *[pltpu.VMEM((rows, LANES), f32)] * 8,
            pltpu.VMEM((devices, 1, LANES), f32),
            pltpu.VMEM((devices, 1, LANES), f32),
            pltpu.SemaphoreType.DMA((6,)),
            pltpu.SemaphoreType.DMA((6,)),
            pltpu.SemaphoreType.DMA,
        ],
        compiler_params=pltpu.CompilerParams(
            collective_id=0, has_side_effects=True, vmem_limit_bytes=48 * 1024 * 1024
        ),
    )(outgoing, stencil_cells, jnp.asarray(lane_parts(table)), jnp.asarray(lane_parts(table.T)), green_spectrum)


def per_device(
    charges,
    projection,
    stencil_block,
    stencil_dest,
    stencil_cells,
    green_spectrum,
    near_blocks,
    near_target,
    near_source,
):
    devices = lax.axis_size(("grp", "slab"))
    sblocks = stencil_block.shape[0]
    capacity = stencil_cells.shape[0] // devices
    panel_rows = charges.reshape(-1, BLK)
    pblocks = panel_rows.shape[0]
    owning = one_hot_rows(stencil_block, pblocks)
    gathered = jnp.dot(owning, panel_rows, precision=highest)
    values = jnp.sum(projection * gathered[:, None, :], axis=2)
    target = stencil_dest[:, 0]
    matches = one_hot_rows(target, devices)
    triangle = (jnp.arange(sblocks)[:, None] >= jnp.arange(sblocks)[None, :]).astype(jnp.float32)
    running = jnp.dot(triangle, matches, precision=highest)
    ranking = (jnp.sum(running * matches, axis=1) - 1.0).astype(jnp.int32)
    position = target * capacity + ranking
    placing = (
        jnp.arange(devices * capacity, dtype=jnp.int32)[:, None] == position[None, :]
    ).astype(jnp.float32)
    outgoing = jnp.dot(placing, values, precision=highest).reshape(devices, 1, capacity * STEN)
    cell_rows = stencil_cells.reshape(devices, 1, capacity * STEN)
    slab = lax.axis_size("slab")
    returned = far_grid(outgoing, cell_rows, green_spectrum, devices, slab).reshape(devices * capacity, STEN)
    at_stencil = lax.dot_general(placing, returned, (((0,), (0,)), ((), ())), precision=highest)
    far_terms = jnp.sum(projection * at_stencil[:, :, None], axis=1)
    far_field = lax.dot_general(owning, far_terms, (((0,), (0,)), ((), ())), precision=highest)
    extended = with_halo(charges, ((("grp", "slab"), 0),), charges.shape[0]).reshape(-1, BLK)
    sources = jnp.dot(one_hot_rows(near_source, extended.shape[0]), extended, precision=highest)
    near_terms = jnp.sum(near_blocks * sources[:, None, :], axis=2)
    receiver = (jnp.arange(pblocks, dtype=jnp.int32)[:, None] == near_target[None, :]).astype(
        jnp.float32
    )
    near_field = jnp.dot(receiver, near_terms, precision=highest)
    return (far_field + near_field).reshape(-1)


def solution(mesh):
    placed = (
        P(("grp", "slab")),
        P(("grp", "slab"), None, None),
        P(("grp", "slab")),
        P(("grp", "slab"), None),
        P(("grp", "slab"), None),
        P(("grp", "slab"), None, None),
        P(("grp", "slab"), None, None),
        P(("grp", "slab")),
        P(("grp", "slab")),
    )
    return jax.shard_map(
        per_device, mesh=mesh, in_specs=placed, out_specs=P(("grp", "slab")), check_vma=False
    )
```

```python
import functools
import math

import jax
import jax.numpy as jnp
import numpy as np
from jax import lax
from jax.experimental import pallas as pl
from jax.experimental.pallas import tpu as pltpu
from jax.sharding import PartitionSpec as P

GX = 256
GY = 256
GZ = 256
BLK = 64
STEN = 64
LANES = 128


NN = (((1,), (0,)), ((), ()))
NT = (((1,), (1,)), ((), ()))


def cas_table(rows, columns, length):
    phase = np.outer(np.arange(rows), np.arange(columns)) % length * (2.0 * math.pi / length)
    return (np.cos(phase) + np.sin(phase)).astype(np.float32)


def lane_parts(table):
    return np.stack(np.split(table, table.shape[1] // LANES, axis=1))


def halves(x):
    top = x.astype(jnp.bfloat16)
    return top, (x - top.astype(jnp.float32)).astype(jnp.bfloat16)


def exact_pick(table, hot, form):
    first = table.astype(jnp.bfloat16)
    second, third = halves(table - first.astype(jnp.float32))
    total = None
    for part in (third, second, first):
        term = lax.dot_general(part, hot, form, preferred_element_type=jnp.float32)
        total = term if total is None else total + term
    return total


def as_bf16(mask):
    return jnp.where(mask, 1.0, 0.0).astype(jnp.bfloat16)


def rows_equal(count, indices):
    return lax.broadcasted_iota(jnp.int32, (count, indices.shape[1]), 0) == indices


def by_parity(pair, indices):
    return jnp.where(lax.bitwise_and(indices, 1) == 0, pair[0:BLK], pair[BLK:])


def to_panels(terms, indices):
    odd = lax.bitwise_and(indices, 1)
    pair = jnp.concatenate([jnp.where(odd == 0, terms, 0.0), jnp.where(odd == 1, terms, 0.0)], axis=0)
    hot = as_bf16(rows_equal(32, lax.shift_right_logical(indices, 1)))
    top, rest = halves(pair)
    return lax.dot_general(hot, top, NT, preferred_element_type=jnp.float32) + lax.dot_general(
        hot, rest, NT, preferred_element_type=jnp.float32
    )


def product(left, right, form):
    def one(a, b):
        return lax.dot_general(a, b, form, preferred_element_type=jnp.float32)

    return one(left[0], right[0]) + one(left[0], right[1]) + one(left[1], right[0])


def whole_kernel(
    devices, slab, charges, block, target, near_target, near_source, cells_t, table, table_t,
    projection_hbm, near_hbm, green_hbm, out,
    rows_hot, cols_hot, weighted, weighted_next, grid_sum, tall, wide, green, left, right, mid, pot,
    recv1, send2a, send2b, recv2a, recv2b, send3a, send3b, recv3a, recv3b, send4, recv4,
    projection, near, halo, turned, cells, square, values, member, terms, sums,
    sends, recvs, halo_sends, halo_recvs, load_sems,
):
    send2, recv2, send3, recv3 = (send2a, send2b), (recv2a, recv2b), (send3a, send3b), (recv3a, recv3b)
    me = lax.axis_index("grp") * slab + lax.axis_index("slab")
    half = devices

    def place(k):
        p = lax.rem(me + k, devices)
        return p, (p // slab, lax.rem(p, slab))

    barrier = pltpu.get_barrier_semaphore()

    def greet(k, carry):
        pl.semaphore_signal(barrier, inc=1, device_id=place(k)[1], device_id_type=pl.DeviceIdType.MESH)
        return carry

    lax.fori_loop(1, devices, greet, 0)
    loads = [
        pltpu.make_async_copy(source, into, load_sems.at[i])
        for i, (source, into) in enumerate(((projection_hbm, projection), (near_hbm, near), (green_hbm, green)))
    ]
    for load in loads:
        load.start()

    turned[:, 0:STEN] = cells_t[...].T
    cells[...] = jnp.concatenate([turned[pl.ds(i, half, stride=2), 0:STEN] for i in range(2)], axis=1)

    hot = as_bf16(rows_equal(32, lax.shift_right_logical(block[...], 1)))
    gathered = by_parity(exact_pick(charges[...].T, hot, NN), block[...])
    loads[0].wait()
    for s in range(STEN):
        terms[s:s + 1, :] = jnp.sum(projection[s] * gathered, axis=0, keepdims=True)
    named = rows_equal(devices, target[...])
    named_hot = as_bf16(named)
    across = (devices, devices)
    earlier = as_bf16(lax.broadcasted_iota(jnp.int32, across, 0) < lax.broadcasted_iota(jnp.int32, across, 1))
    before = lax.dot_general(named_hot, earlier, NN, preferred_element_type=jnp.float32)
    member[0] = as_bf16(named & (before < 0.5))
    member[1] = as_bf16(named & (before > 0.5))
    empty = jnp.zeros((STEN, devices), jnp.bfloat16)
    outgoing = jnp.zeros((devices, 2 * STEN), jnp.float32)
    for part in halves(terms[0:STEN]):
        for slot in range(2):
            spread_part = jnp.concatenate([part, empty] if slot == 0 else [empty, part], axis=0)
            outgoing += lax.dot_general(member[slot], spread_part, NT, preferred_element_type=jnp.float32)
    square[...] = outgoing
    for d in range(devices):
        values[d] = square[d:d + 1, :]

    for h in range(2):
        lanes = slice(h * LANES, (h + 1) * LANES)
        tall[0, :, lanes], tall[1, :, lanes] = halves(table[h])
        for j in range(4):
            chunk = table.at[h][pl.ds(j, half, stride=4), :]
            rows = slice(j * half, (j + 1) * half)
            tall[2, rows, lanes], tall[3, rows, lanes] = halves(chunk)
            wide[0, lanes, rows], wide[1, lanes, rows] = halves(chunk.T)
    for q in range(4):
        lanes = slice(q * LANES, (q + 1) * LANES)
        for xx in range(2):
            chunk = table_t.at[q][pl.ds(xx, half, stride=2), :]
            rows = slice(xx * half, (xx + 1) * half)
            wide[2, rows, lanes], wide[3, rows, lanes] = halves(chunk)
            tall[4, lanes, rows], tall[5, lanes, rows] = halves(chunk.T)

    pl.semaphore_wait(barrier, devices - 1)
    halo_copies = []
    for i, k in enumerate((1, devices - 1)):
        halo_copies.append(pltpu.make_async_remote_copy(
            src_ref=charges, dst_ref=halo.at[i], send_sem=halo_sends.at[i], recv_sem=halo_recvs.at[i],
            device_id=place(k)[1], device_id_type=pl.DeviceIdType.MESH,
        ))

    def row_of(ref, p):
        return ref.at[p]

    def tile_of(ref, p):
        return ref.at[pl.ds(pl.multiple_of(p * 8, 8), 8), :]

    def start_one(number, source, target, view, k):
        p, where = place(k)
        pltpu.make_async_remote_copy(
            src_ref=view(source, p), dst_ref=view(target, me),
            send_sem=sends.at[number], recv_sem=recvs.at[number],
            device_id=where, device_id_type=pl.DeviceIdType.MESH,
        ).start()

    def start_all(number, source, target):
        def start(k, carry):
            start_one(number, source, target, tile_of, k)
            return carry

        lax.fori_loop(1, devices, start, 0)

    def wait_all(ref, sem, view):
        part = ref.at[pl.ds(0, devices - 1)] if view is row_of else ref.at[pl.ds(0, (devices - 1) * 8), :]
        pltpu.make_async_copy(part, part, sem).wait()

    row_id = lax.broadcasted_iota(jnp.int32, (2 * GY, LANES), 0)
    col_id = lax.broadcasted_iota(jnp.int32, (GZ, LANES), 0)

    def mark(e):
        c = e // 8
        lanes = pl.ds(pl.multiple_of(lax.rem(e, 8) * LANES, LANES), LANES)
        cell = cells[pl.ds(e, 1), :]
        row = lax.shift_right_logical(cell, 8)
        col = lax.bitwise_and(cell, 255)
        rows_hot[c, :, lanes] = jnp.where(row_id == row, 1.0, 0.0).astype(jnp.bfloat16)
        cols_hot[c, :, lanes] = jnp.where(col_id == col, 1.0, 0.0).astype(jnp.bfloat16)

    def send_and_mark(k, carry):
        start_one(0, values, recv1, row_of, k)
        mark(k)
        return carry

    lax.fori_loop(1, devices, send_and_mark, 0)
    for copy in halo_copies:
        copy.start()
    mark(0)
    recv1[me] = values[me]
    wait_all(recv1, recvs.at[0], row_of)

    def weigh(c, into):
        for k in range(8):
            lanes = slice(k * LANES, (k + 1) * LANES)
            hot = cols_hot[c, :, lanes]
            top, rest = halves(jnp.broadcast_to(recv1[c * 8 + k], (GZ, LANES)))
            into[0:GZ, lanes] = hot * top
            into[GZ:, lanes] = hot * rest

    def add_chunk(c, weights):
        grid_sum[...] += lax.dot_general(weights[...], rows_hot[c], NT, preferred_element_type=jnp.float32)

    grid_sum[...] = jnp.zeros_like(grid_sum)
    weigh(0, weighted)
    chunks = devices // 8

    def spread(i, carry):
        weigh(2 * i + 1, weighted_next)
        add_chunk(2 * i, weighted)
        weigh(jnp.minimum(2 * i + 2, chunks - 1), weighted)
        add_chunk(2 * i + 1, weighted_next)
        return carry

    lax.fori_loop(0, chunks // 2, spread, 0)

    mine = pl.ds(pl.multiple_of(me * 8, 8), 8)

    def spots(j, xx, h):
        return pl.ds(4 * j + 2 * xx + h, half, stride=8)

    for xx in range(2):
        part = slice(xx * GY, (xx + 1) * GY)
        left[xx], right[xx] = halves(grid_sum[0:GZ, part] + grid_sum[GZ:, part])
    for side in range(2):
        for xx in range(2):
            for j in range(2):
                rows = slice((2 * side + j) * half, (2 * side + j + 1) * half)
                planes = product((tall[2, rows], tall[3, rows]), (left[xx], right[xx]), NN)
                for h in range(2):
                    send2[side][spots(j, xx, h), :] = planes[:, h * LANES:(h + 1) * LANES]
        start_all(1 + side, send2[side], recv2[side])
        recv2[side][mine, :] = send2[side][mine, :]
    for load in loads[1:]:
        load.wait()
    for copy in halo_copies:
        copy.wait()

    inside = [jnp.where(me > 0, halo[0], 0.0), charges[...], jnp.where(me < devices - 1, halo[1], 0.0)]
    read = near_source[...]
    near_hot = as_bf16(rows_equal(96, lax.shift_right_logical(read, 1)))
    picked = by_parity(exact_pick(jnp.concatenate(inside, axis=0).T, near_hot, NN), read)
    for i in range(BLK):
        sums[i:i + 1, :] = jnp.sum(near[i] * picked, axis=0, keepdims=True)
    panels = to_panels(sums[...], near_target[...])

    for side in range(2):
        wait_all(recv2[side], recvs.at[1 + side], tile_of)
        for j in range(2):
            for h in range(2):
                lanes = slice(h * LANES, (h + 1) * LANES)
                for xx in range(2):
                    rows = slice(xx * half, (xx + 1) * half)
                    left[0, rows, lanes], left[1, rows, lanes] = halves(recv2[side][spots(j, xx, h), :])
            total = None
            for b in range(2):
                rows = slice(b * GX, (b + 1) * GX)
                along_x = halves(product((tall[4, rows], tall[5, rows]), (left[0], left[1]), NN))
                spectral = product(along_x, (tall[0], tall[1]), NT)
                scaled = halves(spectral * green[2 * side + j, rows, :])
                back_y = halves(product(scaled, (tall[0], tall[1]), NN))
                term = product((wide[2, :, rows], wide[3, :, rows]), back_y, NN)
                total = term if total is None else total + term
            for h in range(2):
                for xx in range(2):
                    send3[side][spots(j, xx, h), :] = total[xx * half:(xx + 1) * half, h * LANES:(h + 1) * LANES]
        start_all(3 + side, send3[side], recv3[side])
        recv3[side][mine, :] = send3[side][mine, :]

    for side in range(2):
        wait_all(recv3[side], recvs.at[3 + side], tile_of)
        for xx in range(2):
            for j in range(2):
                rows = slice((2 * side + j) * half, (2 * side + j + 1) * half)
                for h in range(2):
                    lanes = slice(xx * GY + h * LANES, xx * GY + (h + 1) * LANES)
                    mid[0, rows, lanes], mid[1, rows, lanes] = halves(recv3[side][spots(j, xx, h), :])
    scale = 1.0 / float(8 * GX * GY * GZ)
    for xx in range(2):
        part = slice(xx * GY, (xx + 1) * GY)
        top, rest = halves(product((wide[0], wide[1]), (mid[0, :, part], mid[1, :, part]), NN) * scale)
        pot[0:GZ, part] = top
        pot[GZ:, part] = rest

    def sample(i, carry):
        c = lax.rem(me // 8 + i, chunks)
        for k in range(4):
            lanes = slice(k * 256, (k + 1) * 256)
            read = lax.dot_general(pot[...], rows_hot[c, :, lanes], NN, preferred_element_type=jnp.float32)
            kept = (read[0:GZ] + read[GZ:]) * cols_hot[c, :, lanes].astype(jnp.float32)
            total = jnp.sum(kept, axis=0, keepdims=True)
            for q in range(2):
                send4[c * 8 + 2 * k + q] = total[:, q * LANES:(q + 1) * LANES]
        return carry

    def send_chunk(i):
        c = lax.rem(me // 8 + i, chunks)
        for q in range(8):
            p = c * 8 + q

            @pl.when(p != me)
            def _():
                start_one(5, send4, recv4, row_of, lax.rem(p + devices - me, devices))

    def sample_and_send(i, carry):
        sample(i, 0)
        send_chunk(i)
        return carry

    lax.fori_loop(0, chunks, sample_and_send, 0)
    recv4[me] = send4[me]
    wait_all(recv4, recvs.at[5], row_of)
    for d in range(devices):
        square[d:d + 1, :] = recv4[d]
    returned = halves(square[...].T)
    at_stencil = jnp.zeros((STEN, devices), jnp.float32)
    for slot in range(2):
        for part in returned:
            at_stencil += lax.dot_general(
                part[slot * STEN:(slot + 1) * STEN], member[slot], NN, preferred_element_type=jnp.float32
            )
    terms[...] = at_stencil
    far = jnp.zeros((BLK, devices), jnp.float32)
    for s in range(STEN):
        far += projection[s] * terms[s:s + 1, :]
    out[...] = panels + to_panels(far, block[...])
    wait_all(values, sends.at[0], row_of)
    for side in range(2):
        wait_all(send2[side], sends.at[1 + side], tile_of)
        wait_all(send3[side], sends.at[3 + side], tile_of)
    wait_all(send4, sends.at[5], row_of)


def per_device(
    slab,
    devices,
    charges,
    projection,
    stencil_block,
    stencil_dest,
    stencil_cells,
    green_spectrum,
    near_blocks,
    near_target,
    near_source,
):
    table = cas_table(2 * GZ, GZ, 2 * GZ)
    vmem = pl.BlockSpec(memory_space=pltpu.VMEM)
    whole = pl.BlockSpec(memory_space=pl.ANY)
    f32, bf16 = jnp.float32, jnp.bfloat16
    rows = devices * 8
    sblocks = stencil_block.shape[0]
    nears = near_target.shape[0]
    panels = (charges.shape[0] // LANES, LANES)
    result = pl.pallas_call(
        functools.partial(whole_kernel, devices, slab),
        out_shape=jax.ShapeDtypeStruct(panels, f32),
        in_specs=[vmem] * 8 + [whole] * 3,
        out_specs=vmem,
        scratch_shapes=[
            pltpu.VMEM((devices // 8, 2 * GY, 8 * LANES), bf16),
            pltpu.VMEM((devices // 8, GZ, 8 * LANES), bf16),
            pltpu.VMEM((2 * GZ, 8 * LANES), bf16),
            pltpu.VMEM((2 * GZ, 8 * LANES), bf16),
            pltpu.VMEM((2 * GZ, 2 * GY), f32),
            pltpu.VMEM((6, 2 * GZ, GZ), bf16),
            pltpu.VMEM((4, GZ, 2 * GZ), bf16),
            pltpu.VMEM((4, 2 * GX, 2 * GY), f32),
            pltpu.VMEM((2, GX, GY), bf16),
            pltpu.VMEM((2, GX, GY), bf16),
            pltpu.VMEM((2, 2 * GZ, 2 * GY), bf16),
            pltpu.VMEM((2 * GZ, 2 * GY), bf16),
            pltpu.VMEM((devices, 1, LANES), f32),
            *[pltpu.VMEM((rows, LANES), f32)] * 8,
            pltpu.VMEM((devices, 1, LANES), f32),
            pltpu.VMEM((devices, 1, LANES), f32),
            pltpu.VMEM((STEN, BLK, sblocks), f32),
            pltpu.VMEM((BLK, BLK, nears), f32),
            pltpu.VMEM((2, *panels), f32),
            pltpu.VMEM((2 * devices, LANES), jnp.int32),
            pltpu.VMEM((devices, LANES), jnp.int32),
            pltpu.VMEM((devices, LANES), f32),
            pltpu.VMEM((devices, 1, LANES), f32),
            pltpu.VMEM((2, devices, sblocks), bf16),
            pltpu.VMEM((STEN, sblocks), f32),
            pltpu.VMEM((BLK, nears), f32),
            pltpu.SemaphoreType.DMA((6,)),
            pltpu.SemaphoreType.DMA((6,)),
            pltpu.SemaphoreType.DMA((2,)),
            pltpu.SemaphoreType.DMA((2,)),
            pltpu.SemaphoreType.DMA((3,)),
        ],
        compiler_params=pltpu.CompilerParams(
            collective_id=0, has_side_effects=True, vmem_limit_bytes=60 * 1024 * 1024
        ),
    )(
        charges.reshape(panels),
        stencil_block.reshape(1, sblocks),
        stencil_dest.reshape(1, sblocks),
        near_target.reshape(1, nears),
        near_source.reshape(1, nears),
        stencil_cells.T,
        jnp.asarray(lane_parts(table)),
        jnp.asarray(lane_parts(table.T)),
        jnp.transpose(projection, (1, 2, 0)),
        jnp.transpose(near_blocks, (1, 2, 0)),
        green_spectrum,
    )
    return result.reshape(-1)


def solution(mesh):
    placed = (
        P(("grp", "slab")),
        P(("grp", "slab"), None, None),
        P(("grp", "slab")),
        P(("grp", "slab"), None),
        P(("grp", "slab"), None),
        P(("grp", "slab"), None, None),
        P(("grp", "slab"), None, None),
        P(("grp", "slab")),
        P(("grp", "slab")),
    )
    return jax.shard_map(
        functools.partial(per_device, mesh.shape["slab"], mesh.size), mesh=mesh, in_specs=placed, out_specs=P(("grp", "slab")), check_vma=False
    )
```
